32 devices in a mesh: dp: 8 (over z, core), tensor: 4 (over y, x).
Axes of the slice: x: 2, y: 2, z: 4, core: 2. Of those that a mesh axis runs over, the one named last changes fastest.
Arguments:
- tokens: bfloat16 [8192, 2048], P(('dp', 'tensor')), may hold values from -6 to 6
- w_qkv: bfloat16 [2048, 6144], P('dp', 'tensor'), may hold values from -0.125 to 0.125
- w_out: bfloat16 [2048, 2048], P('tensor', 'dp'), may hold values from -1 to 1
- w_up: bfloat16 [2048, 8192], P('dp', 'tensor'), may hold values from -0.125 to 0.125
- w_down: bfloat16 [8192, 2048], P('tensor', 'dp'), may hold values from -0.0625 to 0.0625
- w_ada: float32 [256, 8192], P(None, ('dp', 'tensor')), may hold values from -0.1875 to 0.1875
- b_ada: float32 [8192], P(('dp', 'tensor')), may hold values from -1.8 to 1.8
- timesteps: int32 [32], replicated, may hold values from 0 to 999
- image_len: int32 [32], replicated, may hold values from 64 to 1024, as said below
- cotangent: bfloat16 [8192, 2048], P(('dp', 'tensor')), may hold values from -6 to 6
Outputs:
- output: bfloat16 [8192, 2048], P(('dp', 'tensor'))
- grad_input: float32 [8192, 2048], P(('dp', 'tensor'))
- grad_w_qkv: float32 [2048, 6144], P('dp', 'tensor')
- grad_w_out: float32 [2048, 2048], P('tensor', 'dp')
- grad_w_up: float32 [2048, 8192], P('dp', 'tensor')
- grad_w_down: float32 [8192, 2048], P('tensor', 'dp')
- grad_w_ada: float32 [256, 8192], P(None, ('dp', 'tensor'))
- grad_b_ada: float32 [8192], P(('dp', 'tensor'))
The draws below stay inside these ranges and needn't reach their ends.
Inputs may be any that keep to these rules, and one draw needn't show every extreme that they name: `image_len`: 4 images have 1024 tokens, 12 have 1024 // 4 and the rest 1024 // 16; the lengths sum to 8192.
All inputs are finite; a program needn't handle non-finite values.
Results may differ from the reference program's by a relative error of at most 0.012.
Values may be sent and summed in bfloat16 or wider, within the bound.
No kernel may reach another device: no remote copies, remote signals or barrier semaphores. Data moves between devices by JAX's collectives and lax.ppermute only.
A program may use at most 256 MiB of HBM per device.

```python
import math
import jax
import jax.numpy as jnp
from jax import lax

D = 2048
FF = 8192
HEADS = 16
HD = 128
EMB = 256
LONG = 1024
TOKENS = 8192
IMAGES = 32
SHIFT = 32
QB = 512
WIN = 2560


def draw_image_len(key, part):
    order = jax.random.permutation(key, IMAGES).astype(jnp.int32)
    count_long = IMAGES // 8
    count_mid = 3 * IMAGES // 8
    lengths = jnp.where(order < count_long, LONG, jnp.where(order < count_long + count_mid, LONG // 4, LONG // 16))
    return lengths.astype(jnp.int32)


def plant(values, stream_key, least, largest):
    longest = values.shape.index(max(values.shape))
    spots = []
    for shift in (0, 1):
        where = [jax.random.randint(jax.random.fold_in(stream_key, axis), (), 0, length) for axis, length in enumerate(values.shape)]
        where[longest] = (where[longest] + shift) % values.shape[longest]
        spots.append(tuple(where))
    return values.at[spots[0]].set(least).at[spots[1]].set(largest)


def steps_of(rng, shape, cuts, smallest, high):
    factor_of, own = 1.0, jax.random.fold_in(rng, 6)
    for position, blocks in cuts:
        heights = jnp.exp(jax.random.uniform(jax.random.fold_in(own, position), (blocks,), jnp.float32, smallest / len(cuts), high / len(cuts)))
        factor_of = factor_of * jnp.repeat(heights, shape[position] // blocks).reshape([-1 if axis == position else 1 for axis in range(len(shape))])
    return factor_of


def normal_values(rng, extent, width, most, split=(), held_as=jnp.bfloat16):
    array = jax.random.normal(rng, extent, jnp.float32) * width
    if len(split) > 0:
        array = steps_of(rng, extent, split, -0.22, 0.18) * array
    return jnp.clip(array, min=-most, max=most).astype(held_as)


def setup_inputs(seed: int = 0) -> dict:
    splits = jax.random.split(jax.random.key(seed), 11)
    return {
        "tokens": normal_values(splits[0], (TOKENS, D), 1.0, 6.0, ((0, 32),)),
        "w_qkv": normal_values(splits[1], (D, 3 * HEADS * HD), D ** -0.5, 0.125, ((0, 8), (1, 4))),
        "w_out": normal_values(splits[2], (HEADS * HD, D), (D // 64) ** -0.5, 1.0, ((0, 4), (1, 8))),
        "w_up": normal_values(splits[3], (D, FF), D ** -0.5, 0.125, ((0, 8), (1, 4))),
        "w_down": normal_values(splits[4], (FF, D), FF ** -0.5, 0.0625, ((0, 4), (1, 8))),
        "w_ada": normal_values(splits[5], (EMB, 4 * D), (4 * EMB) ** -0.5, 0.1875, ((1, 32),), jnp.float32),
        "b_ada": normal_values(splits[6], (4 * D,), 0.3, 1.8, ((0, 32),), jnp.float32),
        "timesteps": plant(jax.random.randint(splits[7], (IMAGES,), 0, 1000), jax.random.fold_in(splits[7], 1), 0, 999).astype(jnp.int32),
        "image_len": draw_image_len(jax.random.fold_in(splits[10], 71), 0),
        "cotangent": normal_values(splits[9], (TOKENS, D), 1.0, 6.0, ((0, 32),)),
    }


epsilon = 1e-06
highest = lax.Precision.HIGHEST

@jax.custom_vjp
def low(v):
    return lax.optimization_barrier(v.astype(jnp.bfloat16)).astype(jnp.float32)

@jax.custom_vjp
def low_back(v):
    return v

def low_keep(v):
    return (low(v), None)

def low_pass(kept, grad):
    return (grad,)

def back_keep(v):
    return (v, None)

def back_low(kept, grad):
    return (low(grad),)
low.defvjp(low_keep, low_pass)
low_back.defvjp(back_keep, back_low)

def frequency_table(timesteps, columns):
    half_cols = columns // 2
    rates = jnp.exp(-math.log(10000.0) * jnp.arange(half_cols, dtype=jnp.float32) / half_cols)
    angles = timesteps.astype(jnp.float32)[:, None] * rates[None, :]
    return jnp.concatenate([jnp.cos(angles), jnp.sin(angles)], axis=1)

def segment_of(positions, image_len):
    starts = jnp.cumsum(image_len, dtype=jnp.int32) - image_len
    inside = (starts[None, :] <= positions[:, None]).astype(jnp.int32)
    return lax.optimization_barrier(jnp.sum(inside, axis=1, dtype=jnp.int32)) - 1

def norm_mod(rows_in, scale_cols, shift_cols):
    factor = lax.rsqrt(lax.optimization_barrier(jnp.mean(rows_in * rows_in, axis=-1, keepdims=True)) + epsilon)
    return rows_in * factor * (1.0 + scale_cols) + shift_cols

def reference(tokens, w_qkv, w_out, w_up, w_down, w_ada, b_ada, timesteps, image_len, cotangent):
    positions = (jnp.arange(TOKENS, dtype=jnp.int32) + SHIFT) % TOKENS
    segments = segment_of(positions, image_len)
    seg_ext = jnp.concatenate([segments[TOKENS - LONG:], segments, segments[:LONG]])
    freq = frequency_table(timesteps, EMB)
    score_scale = HD ** (-0.5)

    def forward(inputs_f, qkv_w, out_w, up_w, down_w, ada_w, ada_b):
        modulation = jnp.dot(freq, ada_w, precision=highest) + ada_b[None, :]
        mod_tok = modulation[segments]
        scale_one = mod_tok[:, 0:D]
        shift_one = mod_tok[:, D:2 * D]
        scale_two = mod_tok[:, 2 * D:3 * D]
        shift_two = mod_tok[:, 3 * D:4 * D]
        normed_one = low(norm_mod(inputs_f, scale_one, shift_one))
        qkv = low(low_back(jnp.dot(normed_one, qkv_w, precision=highest)))
        qkv = qkv.reshape(TOKENS, HEADS, 3, HD)
        queries = qkv[:, :, 0]
        key_rows = qkv[:, :, 1]
        value_rows = qkv[:, :, 2]
        key_ext = jnp.concatenate([key_rows[TOKENS - LONG:], key_rows, key_rows[:LONG]], axis=0)
        value_ext = jnp.concatenate([value_rows[TOKENS - LONG:], value_rows, value_rows[:LONG]], axis=0)

        def attend(start):
            q_block = lax.dynamic_slice_in_dim(queries, start, QB, 0)
            k_window = lax.dynamic_slice_in_dim(key_ext, start, WIN, 0)
            v_window = lax.dynamic_slice_in_dim(value_ext, start, WIN, 0)
            seg_query = lax.dynamic_slice_in_dim(seg_ext, start + LONG, QB, 0)
            seg_key = lax.dynamic_slice_in_dim(seg_ext, start, WIN, 0)
            scores = low_back(jnp.einsum('qhd,khd->hqk', q_block, k_window, precision=highest) * score_scale)
            same = seg_query[:, None] == seg_key[None, :]
            scores = jnp.where(same[None], scores, -1e+30)
            weights_lo = low(jax.nn.softmax(scores, axis=-1))
            return jnp.einsum('hqk,khd->qhd', weights_lo, v_window, precision=highest)
        starts = jnp.arange(TOKENS // QB, dtype=jnp.int32) * QB
        blocks = lax.map(jax.checkpoint(attend), starts)
        attn = low(low_back(blocks.reshape(TOKENS, HEADS * HD)))
        branch = low_back(jnp.dot(attn, out_w, precision=highest))
        mid_rows = inputs_f + branch
        normed_two = low(norm_mod(mid_rows, scale_two, shift_two))
        up_rows = low_back(jnp.dot(normed_two, up_w, precision=highest))
        act_rows = low(jax.nn.gelu(up_rows, approximate=True))
        mlp_rows = low_back(jnp.dot(act_rows, down_w, precision=highest))
        return mid_rows + mlp_rows
    primals = (tokens.astype(jnp.float32), w_qkv.astype(jnp.float32), w_out.astype(jnp.float32), w_up.astype(jnp.float32), w_down.astype(jnp.float32), w_ada.astype(jnp.float32), b_ada.astype(jnp.float32))
    result, pull = jax.vjp(forward, *primals)
    grads = pull(cotangent.astype(jnp.float32))
    return (result.astype(jnp.bfloat16), grads[0], grads[1], grads[2], grads[3], grads[4], grads[5], grads[6])
```

```python
import math

import jax
import jax.numpy as jnp
from jax import lax
from jax.sharding import PartitionSpec as P

HD = 128
LONG = 1024


epsilon = 1e-06
highest = lax.Precision.HIGHEST


def extended_2(block, sides, width):
    for axis, dim in sides:
        count = lax.axis_size(axis)
        forward = [(i, i + 1) for i in range(count - 1)]
        forward.append((count - 1, 0))
        backward = [(target, source) for source, target in forward]
        low = lax.ppermute(
            lax.slice_in_dim(block, block.shape[dim] - width, None, axis=dim), axis, forward
        )
        high = lax.ppermute(lax.slice_in_dim(block, 0, width, axis=dim), axis, backward)
        block = jnp.concatenate([low, block, high], axis=dim)
    return block


def frequency_table(timesteps, columns):
    half_cols = columns // 2
    rates = jnp.exp(-math.log(10000.0) * jnp.arange(half_cols, dtype=jnp.float32) / half_cols)
    angles = timesteps.astype(jnp.float32)[:, None] * rates[None, :]
    return jnp.concatenate([jnp.cos(angles), jnp.sin(angles)], axis=1)


def segment_of(positions, image_len):
    starts = jnp.cumsum(image_len, dtype=jnp.int32) - image_len
    inside = (starts[None, :] <= positions[:, None]).astype(jnp.int32)
    return jnp.sum(inside, axis=1, dtype=jnp.int32) - 1


def norm_mod(rows_in, scale_cols, shift_cols):
    factor = lax.rsqrt(jnp.mean(rows_in * rows_in, axis=-1, keepdims=True) + epsilon)
    return rows_in * factor * (1.0 + scale_cols) + shift_cols


def gelu_tanh(values):
    return jax.nn.gelu(values, approximate=True)


def fetch_weights(qkv_part, out_part, up_part, down_part):
    return (
        lax.all_gather(qkv_part, "dp", axis=0, tiled=True),
        lax.all_gather(out_part, "dp", axis=1, tiled=True),
        lax.all_gather(up_part, "dp", axis=0, tiled=True),
        lax.all_gather(down_part, "dp", axis=1, tiled=True),
    )


def spread_rows(values):
    return lax.all_gather(values, "tensor", axis=0, tiled=True)


def fold_rows(values):
    low = values.astype(jnp.bfloat16)
    return lax.psum_scatter(low, "tensor", scatter_dimension=0, tiled=True).astype(jnp.float32)


def fold_grad(values, dim):
    low = values.astype(jnp.bfloat16)
    return lax.psum_scatter(low, "dp", scatter_dimension=dim, tiled=True).astype(jnp.float32)


def local(tokens, w_qkv, w_out, w_up, w_down, w_ada, b_ada, timesteps, image_len, cotangent):
    n_tensor = lax.axis_size("tensor")
    n_data = lax.axis_size("dp")
    rows_dev = tokens.shape[0]
    tok_dev = rows_dev * n_tensor
    total_tok = tok_dev * n_data
    shift_pos = LONG // 32
    q_rows = min(512, LONG)
    window = q_rows + 2 * tok_dev
    n_blocks = tok_dev // q_rows
    heads_local = w_qkv.shape[1] // (3 * HD)
    head_cols = heads_local * HD
    score_scale = HD ** (-0.5)
    n_images = image_len.shape[0]
    data_idx = lax.axis_index("dp")
    tensor_idx = lax.axis_index("tensor")
    row_start = (data_idx * n_tensor + tensor_idx) * rows_dev
    row_pos = jnp.mod(row_start + jnp.arange(rows_dev, dtype=jnp.int32) + shift_pos, total_tok)
    seg_rows = segment_of(row_pos, image_len)
    ext_start = data_idx * tok_dev - tok_dev + total_tok
    ext_pos = jnp.mod(ext_start + jnp.arange(3 * tok_dev, dtype=jnp.int32) + shift_pos, total_tok)
    seg_ext = segment_of(ext_pos, image_len)
    full_qkv, full_out, full_up, full_down = fetch_weights(w_qkv, w_out, w_up, w_down)
    freq = frequency_table(timesteps, w_ada.shape[0])
    mod_cols = jnp.dot(freq, w_ada, precision=highest) + b_ada[None, :]
    modulation = lax.all_gather(mod_cols, ("dp", "tensor"), axis=1, tiled=True)
    image_ids = jnp.arange(n_images, dtype=jnp.int32)[None, :]
    onehot_rows = (seg_rows[:, None] == image_ids).astype(jnp.float32)
    mod_rows = jnp.dot(onehot_rows, modulation, precision=highest)
    width = modulation.shape[1] // 4
    scale_one = mod_rows[:, 0:width]
    shift_one = mod_rows[:, width : 2 * width]
    scale_two = mod_rows[:, 2 * width : 3 * width]
    shift_two = mod_rows[:, 3 * width : 4 * width]
    inputs_f = tokens.astype(jnp.float32)
    normed_one = norm_mod(inputs_f, scale_one, shift_one).astype(jnp.bfloat16)
    normed_full = spread_rows(normed_one)
    qkv = jnp.dot(normed_full, full_qkv, preferred_element_type=jnp.float32).astype(jnp.bfloat16)
    qkv = qkv.reshape(tok_dev, heads_local, 3, HD)
    queries = qkv[:, :, 0]
    key_rows = qkv[:, :, 1]
    value_rows = qkv[:, :, 2]
    pair_rows = jnp.concatenate(
        [key_rows.reshape(tok_dev, head_cols), value_rows.reshape(tok_dev, head_cols)], axis=1
    )
    extended = extended_2(pair_rows, (("dp", 0),), tok_dev)
    key_ext = extended[:, :head_cols].reshape(3 * tok_dev, heads_local, HD)
    value_ext = extended[:, head_cols:].reshape(3 * tok_dev, heads_local, HD)

    def block_scores(start_row):
        q_block = queries[start_row : start_row + q_rows]
        k_window = key_ext[start_row : start_row + window]
        raw = (
            jnp.einsum("qhd,khd->hqk", q_block, k_window, preferred_element_type=jnp.float32)
            * score_scale
        )
        seg_query = seg_ext[tok_dev + start_row : tok_dev + start_row + q_rows]
        seg_key = seg_ext[start_row : start_row + window]
        same = seg_query[:, None] == seg_key[None, :]
        return jnp.where(same[None], raw, -1e30)

    out_blocks = []
    log_sums = []
    for block_id in range(n_blocks):
        start_row = block_id * q_rows
        scores = block_scores(start_row)
        row_max = jnp.max(scores, axis=-1, keepdims=True)
        shifted = jnp.exp(scores - row_max)
        row_total = jnp.sum(shifted, axis=-1, keepdims=True)
        weights_lo = (shifted / row_total).astype(jnp.bfloat16)
        log_sums.append(row_max + jnp.log(row_total))
        out_blocks.append(
            jnp.einsum(
                "hqk,khd->qhd",
                weights_lo,
                value_ext[start_row : start_row + window],
                preferred_element_type=jnp.float32,
            )
        )
    attn_f = jnp.concatenate(out_blocks, axis=0)
    attn_lo = attn_f.astype(jnp.bfloat16).reshape(tok_dev, head_cols)
    attn_part = jnp.dot(attn_lo, full_out, preferred_element_type=jnp.float32)
    branch = fold_rows(attn_part)
    mid_rows = inputs_f + branch
    normed_two = norm_mod(mid_rows, scale_two, shift_two).astype(jnp.bfloat16)
    normed_two_full = spread_rows(normed_two)
    up_rows = jnp.dot(normed_two_full, full_up, preferred_element_type=jnp.float32)
    act_rows = gelu_tanh(up_rows).astype(jnp.bfloat16)
    mlp_part = jnp.dot(act_rows, full_down, preferred_element_type=jnp.float32)
    mlp_out = fold_rows(mlp_part)
    result = (mid_rows + mlp_out).astype(jnp.bfloat16)
    grad_rows = cotangent.astype(jnp.float32)
    grad_full = spread_rows(cotangent)
    grad_downw = jnp.einsum("tf,td->fd", act_rows, grad_full, preferred_element_type=jnp.float32)
    d_act = jnp.einsum("td,fd->tf", grad_full, full_down, preferred_element_type=jnp.float32)
    gelu_pull = jax.vjp(gelu_tanh, up_rows)[1]
    d_up = gelu_pull(d_act)[0].astype(jnp.bfloat16)
    grad_upw = jnp.einsum("td,tf->df", normed_two_full, d_up, preferred_element_type=jnp.float32)
    d_h2_part = jnp.einsum("tf,df->td", d_up, full_up, preferred_element_type=jnp.float32)
    d_h2 = fold_rows(d_h2_part)
    norm_two_pull = jax.vjp(norm_mod, mid_rows, scale_two, shift_two)[1]
    d_mid, d_scale_two, d_shift_two = norm_two_pull(d_h2)
    d_mid = grad_rows + d_mid
    branch_full = spread_rows(d_mid.astype(jnp.bfloat16))
    grad_outw = jnp.einsum("tc,td->cd", attn_lo, branch_full, preferred_element_type=jnp.float32)
    d_attn = jnp.einsum("td,cd->tc", branch_full, full_out, preferred_element_type=jnp.float32)
    d_attn = d_attn.astype(jnp.bfloat16).reshape(tok_dev, heads_local, HD)
    d_query_blocks = []
    d_key_ext = jnp.zeros((3 * tok_dev, heads_local, HD), jnp.float32)
    d_value_ext = jnp.zeros((3 * tok_dev, heads_local, HD), jnp.float32)
    for block_id in range(n_blocks):
        start_row = block_id * q_rows
        scores = block_scores(start_row)
        softmax_f = jnp.exp(scores - log_sums[block_id])
        d_out_block = d_attn[start_row : start_row + q_rows]
        q_block = queries[start_row : start_row + q_rows]
        k_window = key_ext[start_row : start_row + window]
        v_window = value_ext[start_row : start_row + window]
        d_soft = jnp.einsum(
            "qhd,khd->hqk", d_out_block, v_window, preferred_element_type=jnp.float32
        )
        inner = jnp.sum(softmax_f * d_soft, axis=-1, keepdims=True)
        d_scores = (softmax_f * (d_soft - inner)).astype(jnp.bfloat16)
        d_query_blocks.append(
            jnp.einsum("hqk,khd->qhd", d_scores, k_window, preferred_element_type=jnp.float32)
            * score_scale
        )
        d_key_ext = d_key_ext.at[start_row : start_row + window].add(
            jnp.einsum("hqk,qhd->khd", d_scores, q_block, preferred_element_type=jnp.float32)
            * score_scale
        )
        d_value_ext = d_value_ext.at[start_row : start_row + window].add(
            jnp.einsum(
                "hqk,qhd->khd",
                softmax_f.astype(jnp.bfloat16),
                d_out_block,
                preferred_element_type=jnp.float32,
            )
        )
    stacked = jnp.concatenate(
        [d_key_ext.reshape(3 * tok_dev, head_cols), d_value_ext.reshape(3 * tok_dev, head_cols)],
        axis=1,
    )
    outer_rows = jnp.concatenate([stacked[:tok_dev], stacked[2 * tok_dev :]], axis=0)
    returned = extended_2(outer_rows.astype(jnp.bfloat16), (("dp", 0),), tok_dev).astype(
        outer_rows.dtype
    )
    own_grads = stacked[tok_dev : 2 * tok_dev] + returned[:tok_dev] + returned[3 * tok_dev :]
    d_query = jnp.concatenate(d_query_blocks, axis=0)
    d_key = own_grads[:, :head_cols].reshape(tok_dev, heads_local, HD)
    d_value = own_grads[:, head_cols:].reshape(tok_dev, heads_local, HD)
    d_qkv = (
        jnp.stack([d_query, d_key, d_value], axis=2)
        .astype(jnp.bfloat16)
        .reshape(tok_dev, 3 * head_cols)
    )
    grad_qkvw = jnp.einsum("td,tc->dc", normed_full, d_qkv, preferred_element_type=jnp.float32)
    d_h1_part = jnp.einsum("tc,dc->td", d_qkv, full_qkv, preferred_element_type=jnp.float32)
    d_h1 = fold_rows(d_h1_part)
    norm_one_pull = jax.vjp(norm_mod, inputs_f, scale_one, shift_one)[1]
    d_inputs, d_scale_one, d_shift_one = norm_one_pull(d_h1)
    grad_input = d_mid + d_inputs
    d_mod_rows = jnp.concatenate([d_scale_one, d_shift_one, d_scale_two, d_shift_two], axis=1)
    d_mod = jnp.dot(onehot_rows.T, d_mod_rows, precision=highest)
    d_mod_cols = lax.psum_scatter(d_mod, ("dp", "tensor"), scatter_dimension=1, tiled=True)
    grad_adaw = jnp.dot(freq.T, d_mod_cols, precision=highest)
    grad_bias = jnp.sum(d_mod_cols, axis=0)
    grad_qkvw, grad_outw, grad_upw, grad_downw = (
        fold_grad(grad_qkvw, 0),
        fold_grad(grad_outw, 1),
        fold_grad(grad_upw, 0),
        fold_grad(grad_downw, 1),
    )
    return (result, grad_input, grad_qkvw, grad_outw, grad_upw, grad_downw, grad_adaw, grad_bias)


def solution(mesh):
    in_specs = (
        P(("dp", "tensor"), None),
        P("dp", "tensor"),
        P("tensor", "dp"),
        P("dp", "tensor"),
        P("tensor", "dp"),
        P(None, ("dp", "tensor")),
        P(("dp", "tensor")),
        P(),
        P(),
        P(("dp", "tensor"), None),
    )
    out_specs = (
        P(("dp", "tensor"), None),
        P(("dp", "tensor"), None),
        P("dp", "tensor"),
        P("tensor", "dp"),
        P("dp", "tensor"),
        P("tensor", "dp"),
        P(None, ("dp", "tensor")),
        P(("dp", "tensor")),
    )
    return jax.shard_map(local, mesh=mesh, in_specs=in_specs, out_specs=out_specs, check_vma=False)
```

```python
import math

import jax
import jax.numpy as jnp
from jax import lax
from jax.sharding import PartitionSpec as P

HD = 128
LONG = 1024


epsilon = 1e-06
highest = lax.Precision.HIGHEST


def extended_2(block, sides, width):
    for axis, dim in sides:
        count = lax.axis_size(axis)
        forward = [(i, i + 1) for i in range(count - 1)]
        forward.append((count - 1, 0))
        backward = [(target, source) for source, target in forward]
        low = lax.ppermute(
            lax.slice_in_dim(block, block.shape[dim] - width, None, axis=dim), axis, forward
        )
        high = lax.ppermute(lax.slice_in_dim(block, 0, width, axis=dim), axis, backward)
        block = jnp.concatenate([low, block, high], axis=dim)
    return block


def frequency_table(timesteps, columns):
    half_cols = columns // 2
    rates = jnp.exp(-math.log(10000.0) * jnp.arange(half_cols, dtype=jnp.float32) / half_cols)
    angles = timesteps.astype(jnp.float32)[:, None] * rates[None, :]
    return jnp.concatenate([jnp.cos(angles), jnp.sin(angles)], axis=1)


def segment_of(positions, image_len):
    starts = jnp.cumsum(image_len, dtype=jnp.int32) - image_len
    inside = (starts[None, :] <= positions[:, None]).astype(jnp.int32)
    return jnp.sum(inside, axis=1, dtype=jnp.int32) - 1


def norm_mod(rows_in, scale_cols, shift_cols):
    factor = lax.rsqrt(jnp.mean(rows_in * rows_in, axis=-1, keepdims=True) + epsilon)
    return rows_in * factor * (1.0 + scale_cols) + shift_cols


def gelu_tanh(values):
    return jax.nn.gelu(values, approximate=True)


def fetch_weights(qkv_part, out_part, up_part, down_part):
    return (
        lax.all_gather(qkv_part, "dp", axis=0, tiled=True),
        lax.all_gather(out_part, "dp", axis=1, tiled=True),
        lax.all_gather(up_part, "dp", axis=0, tiled=True),
        lax.all_gather(down_part, "dp", axis=1, tiled=True),
    )


def swap(values, axis, bit):
    count = lax.axis_size(axis)
    return lax.ppermute(values, axis, [(i, i ^ bit) for i in range(count)])


def spread_rows(values):
    count = lax.axis_size("tensor")
    if count != 4:
        others = [swap(values, "tensor", k) for k in range(1, count)]
        return jnp.concatenate([values] + others, axis=0)
    half = values.shape[0] // 2
    from_one = swap(values, "tensor", 1)
    from_two = swap(values, "tensor", 2)
    far_low = swap(from_two[:half], "tensor", 1)
    far_high = swap(from_one[half:], "tensor", 2)
    return jnp.concatenate([values, from_one, from_two, far_low, far_high], axis=0)


def fold_rows(values):
    count = lax.axis_size("tensor")
    rows = values.shape[0] // count
    if count != 4:
        total = values[:rows]
        for k in range(1, count):
            part = values[k * rows : (k + 1) * rows].astype(jnp.bfloat16)
            total = total + swap(part, "tensor", k).astype(jnp.float32)
        return total
    half = rows // 2
    own, one, two, far = (values[k * rows : (k + 1) * rows] for k in range(4))
    low = jnp.bfloat16
    far_low = swap(far[:half].astype(low), "tensor", 1).astype(jnp.float32)
    far_high = swap(far[half:].astype(low), "tensor", 2).astype(jnp.float32)
    two = jnp.concatenate([two[:half] + far_low, two[half:]], axis=0).astype(low)
    one = jnp.concatenate([one[:half], one[half:] + far_high], axis=0).astype(low)
    from_one = swap(one, "tensor", 1).astype(jnp.float32)
    from_two = swap(two, "tensor", 2).astype(jnp.float32)
    return own + from_one + from_two


def place_rows(values, tensor_idx):
    count = lax.axis_size("tensor")
    rows = values.shape[0] // count
    chunks = [values[k * rows : (k + 1) * rows] for k in range(count)]
    for bit in bits_of("tensor"):
        flip = (tensor_idx & bit) != 0
        chunks = [jnp.where(flip, chunks[k ^ bit], chunks[k]) for k in range(count)]
    return jnp.concatenate(chunks, axis=0)


def bits_of(axis):
    count = lax.axis_size(axis)
    return [1 << k for k in range(count.bit_length() - 1)]


def spread_columns(values):
    rows, cols = values.shape
    sides = [("dp", b) for b in reversed(bits_of("dp"))]
    sides += [("tensor", b) for b in reversed(bits_of("tensor"))]
    for axis, bit in sides:
        other = swap(values, axis, bit)
        high = (lax.axis_index(axis) & bit) != 0
        values = jnp.stack([jnp.where(high, other, values), jnp.where(high, values, other)])
    count = len(sides)
    order = (count,) + tuple(reversed(range(count))) + (count + 1,)
    return values.transpose(order).reshape(rows, -1)


def fold_columns(values):
    sides = [("dp", b) for b in reversed(bits_of("dp"))]
    sides += [("tensor", b) for b in reversed(bits_of("tensor"))]
    count = len(sides)
    rows = values.shape[0]
    values = values.reshape((rows,) + (2,) * count + (-1,))
    order = tuple(reversed(range(1, count + 1))) + (0, count + 1)
    values = values.transpose(order)
    for axis, bit in reversed(sides):
        high = (lax.axis_index(axis) & bit) != 0
        kept = jnp.where(high, values[1], values[0])
        given = jnp.where(high, values[0], values[1])
        values = kept + swap(given, axis, bit)
    return values


def fold_grad(values, dim):
    low = values.astype(jnp.bfloat16)
    return lax.psum_scatter(low, "dp", scatter_dimension=dim, tiled=True).astype(jnp.float32)


def local(tokens, w_qkv, w_out, w_up, w_down, w_ada, b_ada, timesteps, image_len, cotangent):
    n_tensor = lax.axis_size("tensor")
    n_data = lax.axis_size("dp")
    rows_dev = tokens.shape[0]
    tok_dev = rows_dev * n_tensor
    total_tok = tok_dev * n_data
    shift_pos = LONG // 32
    q_rows = min(512, LONG)
    window = q_rows + 2 * tok_dev
    n_blocks = tok_dev // q_rows
    heads_local = w_qkv.shape[1] // (3 * HD)
    head_cols = heads_local * HD
    score_scale = HD ** (-0.5)
    n_images = image_len.shape[0]
    data_idx = lax.axis_index("dp")
    tensor_idx = lax.axis_index("tensor")
    row_start = (data_idx * n_tensor + tensor_idx) * rows_dev
    row_pos = jnp.mod(row_start + jnp.arange(rows_dev, dtype=jnp.int32) + shift_pos, total_tok)
    seg_rows = segment_of(row_pos, image_len)
    ext_start = data_idx * tok_dev - tok_dev + total_tok
    ext_pos = jnp.mod(ext_start + jnp.arange(3 * tok_dev, dtype=jnp.int32) + shift_pos, total_tok)
    seg_ext = segment_of(ext_pos, image_len)
    full_qkv, full_out, full_up, full_down = fetch_weights(w_qkv, w_out, w_up, w_down)
    freq = frequency_table(timesteps, w_ada.shape[0])
    mod_cols = jnp.dot(freq, w_ada, precision=highest) + b_ada[None, :]
    modulation = spread_columns(mod_cols)
    image_ids = jnp.arange(n_images, dtype=jnp.int32)[None, :]
    onehot_rows = (seg_rows[:, None] == image_ids).astype(jnp.float32)
    mod_rows = jnp.dot(onehot_rows, modulation, precision=highest)
    width = modulation.shape[1] // 4
    scale_one = mod_rows[:, 0:width]
    shift_one = mod_rows[:, width : 2 * width]
    scale_two = mod_rows[:, 2 * width : 3 * width]
    shift_two = mod_rows[:, 3 * width : 4 * width]
    inputs_f = tokens.astype(jnp.float32)
    normed_one = norm_mod(inputs_f, scale_one, shift_one).astype(jnp.bfloat16)
    normed_full = spread_rows(normed_one)
    qkv = jnp.dot(normed_full, full_qkv, preferred_element_type=jnp.float32).astype(jnp.bfloat16)
    qkv = place_rows(qkv, tensor_idx).reshape(tok_dev, heads_local, 3, HD)
    queries = qkv[:, :, 0]
    key_rows = qkv[:, :, 1]
    value_rows = qkv[:, :, 2]
    pair_rows = jnp.concatenate(
        [key_rows.reshape(tok_dev, head_cols), value_rows.reshape(tok_dev, head_cols)], axis=1
    )
    extended = extended_2(pair_rows, (("dp", 0),), tok_dev)
    key_ext = extended[:, :head_cols].reshape(3 * tok_dev, heads_local, HD)
    value_ext = extended[:, head_cols:].reshape(3 * tok_dev, heads_local, HD)

    def block_scores(start_row):
        q_block = queries[start_row : start_row + q_rows]
        k_window = key_ext[start_row : start_row + window]
        raw = (
            jnp.einsum("qhd,khd->hqk", q_block, k_window, preferred_element_type=jnp.float32)
            * score_scale
        )
        seg_query = seg_ext[tok_dev + start_row : tok_dev + start_row + q_rows]
        seg_key = seg_ext[start_row : start_row + window]
        same = seg_query[:, None] == seg_key[None, :]
        return jnp.where(same[None], raw, -1e30)

    out_blocks = []
    log_sums = []
    for block_id in range(n_blocks):
        start_row = block_id * q_rows
        scores = block_scores(start_row)
        row_max = jnp.max(scores, axis=-1, keepdims=True)
        shifted = jnp.exp(scores - row_max)
        row_total = jnp.sum(shifted, axis=-1, keepdims=True)
        weights_lo = (shifted / row_total).astype(jnp.bfloat16)
        log_sums.append(row_max + jnp.log(row_total))
        out_blocks.append(
            jnp.einsum(
                "hqk,khd->qhd",
                weights_lo,
                value_ext[start_row : start_row + window],
                preferred_element_type=jnp.float32,
            )
        )
    attn_f = jnp.concatenate(out_blocks, axis=0)
    attn_lo = place_rows(attn_f.astype(jnp.bfloat16).reshape(tok_dev, head_cols), tensor_idx)
    attn_part = jnp.dot(attn_lo, full_out, preferred_element_type=jnp.float32)
    branch = fold_rows(attn_part)
    mid_rows = inputs_f + branch
    normed_two = norm_mod(mid_rows, scale_two, shift_two).astype(jnp.bfloat16)
    normed_two_full = spread_rows(normed_two)
    up_rows = jnp.dot(normed_two_full, full_up, preferred_element_type=jnp.float32)
    act_rows = gelu_tanh(up_rows).astype(jnp.bfloat16)
    mlp_part = jnp.dot(act_rows, full_down, preferred_element_type=jnp.float32)
    mlp_out = fold_rows(mlp_part)
    result = (mid_rows + mlp_out).astype(jnp.bfloat16)
    grad_rows = cotangent.astype(jnp.float32)
    grad_full = spread_rows(cotangent)
    grad_downw = jnp.einsum("tf,td->fd", act_rows, grad_full, preferred_element_type=jnp.float32)
    d_act = jnp.einsum("td,fd->tf", grad_full, full_down, preferred_element_type=jnp.float32)
    gelu_pull = jax.vjp(gelu_tanh, up_rows)[1]
    d_up = gelu_pull(d_act)[0].astype(jnp.bfloat16)
    grad_upw = jnp.einsum("td,tf->df", normed_two_full, d_up, preferred_element_type=jnp.float32)
    d_h2_part = jnp.einsum("tf,df->td", d_up, full_up, preferred_element_type=jnp.float32)
    d_h2 = fold_rows(d_h2_part)
    norm_two_pull = jax.vjp(norm_mod, mid_rows, scale_two, shift_two)[1]
    d_mid, d_scale_two, d_shift_two = norm_two_pull(d_h2)
    d_mid = grad_rows + d_mid
    branch_full = spread_rows(d_mid.astype(jnp.bfloat16))
    grad_outw = jnp.einsum("tc,td->cd", attn_lo, branch_full, preferred_element_type=jnp.float32)
    d_attn = jnp.einsum("td,cd->tc", branch_full, full_out, preferred_element_type=jnp.float32)
    d_attn = place_rows(d_attn.astype(jnp.bfloat16), tensor_idx).reshape(tok_dev, heads_local, HD)
    d_query_blocks = []
    d_key_ext = jnp.zeros((3 * tok_dev, heads_local, HD), jnp.float32)
    d_value_ext = jnp.zeros((3 * tok_dev, heads_local, HD), jnp.float32)
    for block_id in range(n_blocks):
        start_row = block_id * q_rows
        scores = block_scores(start_row)
        softmax_f = jnp.exp(scores - log_sums[block_id])
        d_out_block = d_attn[start_row : start_row + q_rows]
        q_block = queries[start_row : start_row + q_rows]
        k_window = key_ext[start_row : start_row + window]
        v_window = value_ext[start_row : start_row + window]
        d_soft = jnp.einsum(
            "qhd,khd->hqk", d_out_block, v_window, preferred_element_type=jnp.float32
        )
        inner = jnp.sum(softmax_f * d_soft, axis=-1, keepdims=True)
        d_scores = (softmax_f * (d_soft - inner)).astype(jnp.bfloat16)
        d_query_blocks.append(
            jnp.einsum("hqk,khd->qhd", d_scores, k_window, preferred_element_type=jnp.float32)
            * score_scale
        )
        d_key_ext = d_key_ext.at[start_row : start_row + window].add(
            jnp.einsum("hqk,qhd->khd", d_scores, q_block, preferred_element_type=jnp.float32)
            * score_scale
        )
        d_value_ext = d_value_ext.at[start_row : start_row + window].add(
            jnp.einsum(
                "hqk,qhd->khd",
                softmax_f.astype(jnp.bfloat16),
                d_out_block,
                preferred_element_type=jnp.float32,
            )
        )
    stacked = jnp.concatenate(
        [d_key_ext.reshape(3 * tok_dev, head_cols), d_value_ext.reshape(3 * tok_dev, head_cols)],
        axis=1,
    )
    outer_rows = jnp.concatenate([stacked[:tok_dev], stacked[2 * tok_dev :]], axis=0)
    returned = extended_2(outer_rows.astype(jnp.bfloat16), (("dp", 0),), tok_dev).astype(
        outer_rows.dtype
    )
    own_grads = stacked[tok_dev : 2 * tok_dev] + returned[:tok_dev] + returned[3 * tok_dev :]
    d_query = jnp.concatenate(d_query_blocks, axis=0)
    d_key = own_grads[:, :head_cols].reshape(tok_dev, heads_local, HD)
    d_value = own_grads[:, head_cols:].reshape(tok_dev, heads_local, HD)
    d_qkv = (
        jnp.stack([d_query, d_key, d_value], axis=2)
        .astype(jnp.bfloat16)
        .reshape(tok_dev, 3 * head_cols)
    )
    d_qkv = place_rows(d_qkv, tensor_idx)
    grad_qkvw = jnp.einsum("td,tc->dc", normed_full, d_qkv, preferred_element_type=jnp.float32)
    d_h1_part = jnp.einsum("tc,dc->td", d_qkv, full_qkv, preferred_element_type=jnp.float32)
    d_h1 = fold_rows(d_h1_part)
    norm_one_pull = jax.vjp(norm_mod, inputs_f, scale_one, shift_one)[1]
    d_inputs, d_scale_one, d_shift_one = norm_one_pull(d_h1)
    grad_input = d_mid + d_inputs
    d_mod_rows = jnp.concatenate([d_scale_one, d_shift_one, d_scale_two, d_shift_two], axis=1)
    d_mod = jnp.dot(onehot_rows.T, d_mod_rows, precision=highest)
    d_mod_cols = fold_columns(d_mod)
    grad_adaw = jnp.dot(freq.T, d_mod_cols, precision=highest)
    grad_bias = jnp.sum(d_mod_cols, axis=0)
    grad_qkvw, grad_outw, grad_upw, grad_downw = (
        fold_grad(grad_qkvw, 0),
        fold_grad(grad_outw, 1),
        fold_grad(grad_upw, 0),
        fold_grad(grad_downw, 1),
    )
    return (result, grad_input, grad_qkvw, grad_outw, grad_upw, grad_downw, grad_adaw, grad_bias)


def solution(mesh):
    in_specs = (
        P(("dp", "tensor"), None),
        P("dp", "tensor"),
        P("tensor", "dp"),
        P("dp", "tensor"),
        P("tensor", "dp"),
        P(None, ("dp", "tensor")),
        P(("dp", "tensor")),
        P(),
        P(),
        P(("dp", "tensor"), None),
    )
    out_specs = (
        P(("dp", "tensor"), None),
        P(("dp", "tensor"), None),
        P("dp", "tensor"),
        P("tensor", "dp"),
        P("dp", "tensor"),
        P("tensor", "dp"),
        P(None, ("dp", "tensor")),
        P(("dp", "tensor")),
    )
    return jax.shard_map(local, mesh=mesh, in_specs=in_specs, out_specs=out_specs, check_vma=False)
```

```python
import functools
import math

import jax
import jax.numpy as jnp
from jax import lax
from jax.experimental import pallas as pl
from jax.experimental.pallas import tpu as pltpu
from jax.sharding import PartitionSpec as P

HD = 128
LONG = 1024


epsilon = 1e-06
highest = lax.Precision.HIGHEST


LOG2E = 1.4426950408889634


def dot_of(left, right, dims):
    return lax.dot_general(left, right, ((dims[:1], dims[1:]), ((), ())), preferred_element_type=jnp.float32)


def tile_at(index, scalars, n_tensor):
    return (index // n_tensor) * n_tensor + jnp.bitwise_xor(index % n_tensor, scalars[0])


def attend_body(heads, n_q, n_tensor, scalars, q_ref, kv_ref, seg_k_ref, seg_q_ref, out_ref, lse_ref, acc_ref, max_ref, sum_ref):
    tile = q_ref.shape[0]
    step = pl.program_id(0)
    factor = HD ** (-0.5) * LOG2E
    acc_ref[...] = jnp.zeros_like(acc_ref)
    max_ref[...] = jnp.full_like(max_ref, -1e30)
    sum_ref[...] = jnp.zeros_like(sum_ref)

    def visit(index, carry):
        start = pl.multiple_of(tile_at(index, scalars, n_tensor) * tile, tile)
        logical = pl.multiple_of(index * tile, tile)
        same = seg_k_ref[pl.ds(logical, tile), :] == seg_q_ref[0]
        for h in range(heads):
            keys = kv_ref[pl.ds(start, tile), 2 * h * HD : (2 * h + 1) * HD]
            vals = kv_ref[pl.ds(start, tile), (2 * h + 1) * HD : (2 * h + 2) * HD]
            query = q_ref[:, 3 * h * HD : (3 * h + 1) * HD]
            scores = jnp.where(same, dot_of(keys, query, (1, 1)) * factor, -1e30)
            old = max_ref[h]
            top = jnp.maximum(old, jnp.max(scores, axis=0, keepdims=True))
            weights = jnp.exp2(scores - top)
            shrink = jnp.exp2(old - top)
            sum_ref[h] = sum_ref[h] * shrink + jnp.sum(weights, axis=0, keepdims=True)
            acc_ref[h] = acc_ref[h] * shrink + dot_of(vals, weights.astype(jnp.bfloat16), (0, 0))
            max_ref[h] = top
        return carry

    lax.fori_loop(scalars[1 + step], scalars[1 + n_q + step], visit, 0)
    for h in range(heads):
        out_ref[:, h * HD : (h + 1) * HD] = (acc_ref[h] / sum_ref[h]).T.astype(jnp.bfloat16)
        lse_ref[0, h] = (max_ref[h] + jnp.log2(sum_ref[h]))[0]


def attend(scalars, qkv, kv_ext, seg_k, seg_q, n_tensor):
    rows, cols = qkv.shape
    heads = cols // (3 * HD)
    tile = rows // n_tensor
    own = lambda i, s: (jnp.bitwise_xor(i, s[0]), 0)
    grid_spec = pltpu.PrefetchScalarGridSpec(
        num_scalar_prefetch=1,
        grid=(n_tensor,),
        in_specs=[
            pl.BlockSpec((tile, cols), own),
            pl.BlockSpec(kv_ext.shape, lambda i, s: (0, 0)),
            pl.BlockSpec(seg_k.shape, lambda i, s: (0, 0)),
            pl.BlockSpec((1, 1, tile), lambda i, s: (i, 0, 0)),
        ],
        out_specs=[
            pl.BlockSpec((tile, heads * HD), own),
            pl.BlockSpec((1, heads, tile), lambda i, s: (i, 0, 0)),
        ],
        scratch_shapes=[
            pltpu.VMEM((heads, HD, tile), jnp.float32),
            pltpu.VMEM((heads, 1, tile), jnp.float32),
            pltpu.VMEM((heads, 1, tile), jnp.float32),
        ],
    )
    return pl.pallas_call(
        functools.partial(attend_body, heads, n_tensor, n_tensor),
        grid_spec=grid_spec,
        out_shape=[
            jax.ShapeDtypeStruct((rows, heads * HD), jnp.bfloat16),
            jax.ShapeDtypeStruct((n_tensor, heads, tile), jnp.float32),
        ],
        compiler_params=pltpu.CompilerParams(vmem_limit_bytes=48 * 1024 * 1024),
        name="attend",
    )(scalars, qkv, kv_ext, seg_k, seg_q)


def pull_body(heads, n_q, n_tensor, scalars, q_ref, kv_ref, seg_k_ref, seg_q_ref, lse_ref, attn_ref, grad_ref, dq_ref, low_ref, own_ref, high_ref, dq_acc, dkv_acc):
    tile = q_ref.shape[0]
    rows = n_q * tile
    step = pl.program_id(0)
    scale = HD ** (-0.5)

    @pl.when(step == 0)
    def _():
        dkv_acc[...] = jnp.zeros_like(dkv_acc)

    dq_acc[...] = jnp.zeros_like(dq_acc)
    inner = []
    for h in range(heads):
        part = slice(h * HD, (h + 1) * HD)
        product = grad_ref[:, part].astype(jnp.float32) * attn_ref[:, part].astype(jnp.float32)
        inner.append(jnp.sum(product.T, axis=0, keepdims=True))

    def visit(index, carry):
        start = pl.multiple_of(tile_at(index, scalars, n_tensor) * tile, tile)
        logical = pl.multiple_of(index * tile, tile)
        same = seg_k_ref[pl.ds(logical, tile), :] == seg_q_ref[0]
        for h in range(heads):
            k_part = slice(2 * h * HD, (2 * h + 1) * HD)
            v_part = slice((2 * h + 1) * HD, (2 * h + 2) * HD)
            keys = kv_ref[pl.ds(start, tile), k_part]
            vals = kv_ref[pl.ds(start, tile), v_part]
            query = q_ref[:, 3 * h * HD : (3 * h + 1) * HD]
            grad = grad_ref[:, h * HD : (h + 1) * HD]
            scores = dot_of(keys, query, (1, 1)) * (scale * LOG2E)
            probs = jnp.exp2(jnp.where(same, scores - lse_ref[0, h : h + 1, :], -1e30))
            d_probs = dot_of(vals, grad, (1, 1))
            d_scores = (probs * (d_probs - inner[h])).astype(jnp.bfloat16)
            dkv_acc[pl.ds(start, tile), v_part] += dot_of(probs.astype(jnp.bfloat16), grad, (1, 0))
            dkv_acc[pl.ds(start, tile), k_part] += dot_of(d_scores, query, (1, 0))
            dq_acc[h] += dot_of(d_scores, keys, (0, 0))
        return carry

    lax.fori_loop(scalars[1 + step], scalars[1 + n_q + step], visit, 0)
    for h in range(heads):
        dq_ref[:, h * HD : (h + 1) * HD] = (dq_acc[h] * scale).astype(jnp.bfloat16)

    @pl.when(step == n_q - 1)
    def _():
        for h in range(2 * heads):
            part = slice(h * HD, (h + 1) * HD)
            factor = scale if h % 2 == 0 else 1.0
            low_ref[:, part] = (dkv_acc[0:rows, part] * factor).astype(jnp.bfloat16)
            own_ref[:, part] = dkv_acc[rows : 2 * rows, part] * factor
            high_ref[:, part] = (dkv_acc[2 * rows : 3 * rows, part] * factor).astype(jnp.bfloat16)


def pull(scalars, qkv, kv_ext, seg_k, seg_q, lse, attn, grad, n_tensor):
    rows, cols = qkv.shape
    heads = cols // (3 * HD)
    tile = rows // n_tensor
    own = lambda i, s: (jnp.bitwise_xor(i, s[0]), 0)
    whole = lambda i, s: (0, 0)
    kv_shape = (rows, 2 * heads * HD)
    grid_spec = pltpu.PrefetchScalarGridSpec(
        num_scalar_prefetch=1,
        grid=(n_tensor,),
        in_specs=[
            pl.BlockSpec((tile, cols), own),
            pl.BlockSpec(kv_ext.shape, whole),
            pl.BlockSpec(seg_k.shape, whole),
            pl.BlockSpec((1, 1, tile), lambda i, s: (i, 0, 0)),
            pl.BlockSpec((1, heads, tile), lambda i, s: (i, 0, 0)),
            pl.BlockSpec((tile, heads * HD), own),
            pl.BlockSpec((tile, heads * HD), own),
        ],
        out_specs=[pl.BlockSpec((tile, heads * HD), own)] + [pl.BlockSpec(kv_shape, whole)] * 3,
        scratch_shapes=[
            pltpu.VMEM((heads, tile, HD), jnp.float32),
            pltpu.VMEM(kv_ext.shape, jnp.float32),
        ],
    )
    return pl.pallas_call(
        functools.partial(pull_body, heads, n_tensor, n_tensor),
        grid_spec=grid_spec,
        out_shape=[
            jax.ShapeDtypeStruct((rows, heads * HD), jnp.bfloat16),
            jax.ShapeDtypeStruct(kv_shape, jnp.bfloat16),
            jax.ShapeDtypeStruct(kv_shape, jnp.float32),
            jax.ShapeDtypeStruct(kv_shape, jnp.bfloat16),
        ],
        compiler_params=pltpu.CompilerParams(vmem_limit_bytes=58 * 1024 * 1024),
        name="attend_pull",
    )(scalars, qkv, kv_ext, seg_k, seg_q, lse, attn, grad)


def ring(axis):
    count = lax.axis_size(axis)
    return [(i, (i + 1) % count) for i in range(count)], [((i + 1) % count, i) for i in range(count)]


def tie(values, *others):
    return lax.optimization_barrier((values,) + others)[0]


def frequency_table(timesteps, columns):
    half_cols = columns // 2
    rates = jnp.exp(-math.log(10000.0) * jnp.arange(half_cols, dtype=jnp.float32) / half_cols)
    angles = timesteps.astype(jnp.float32)[:, None] * rates[None, :]
    return jnp.concatenate([jnp.cos(angles), jnp.sin(angles)], axis=1)


def segment_of(positions, image_len):
    starts = jnp.cumsum(image_len, dtype=jnp.int32) - image_len
    inside = (starts[None, :] <= positions[:, None]).astype(jnp.int32)
    return jnp.sum(inside, axis=1, dtype=jnp.int32) - 1


def norm_mod(rows_in, scale_cols, shift_cols):
    factor = lax.rsqrt(jnp.mean(rows_in * rows_in, axis=-1, keepdims=True) + epsilon)
    return rows_in * factor * (1.0 + scale_cols) + shift_cols


def gelu_tanh(values):
    return jax.nn.gelu(values, approximate=True)


def swap(values, axis, bit):
    count = lax.axis_size(axis)
    return lax.ppermute(values, axis, [(i, i ^ bit) for i in range(count)])


def spread_rows(values):
    count = lax.axis_size("tensor")
    if count != 4:
        others = [swap(values, "tensor", k) for k in range(1, count)]
        return jnp.concatenate([values] + others, axis=0)
    half = values.shape[0] // 2
    from_one = swap(values, "tensor", 1)
    from_two = swap(values, "tensor", 2)
    far_low = swap(from_two[:half], "tensor", 1)
    far_high = swap(from_one[half:], "tensor", 2)
    return jnp.concatenate([values, from_one, from_two, far_low, far_high], axis=0)


def fold_rows(values, also=()):
    count = lax.axis_size("tensor")
    rows = values.shape[0] // count
    if count != 4:
        total = values[:rows]
        for k in range(1, count):
            part = values[k * rows : (k + 1) * rows].astype(jnp.bfloat16)
            total = total + swap(part, "tensor", k).astype(jnp.float32)
        return total
    half = rows // 2
    own, one, two, far = (values[k * rows : (k + 1) * rows] for k in range(4))
    low = jnp.bfloat16
    far_low = swap(far[:half].astype(low), "tensor", 1).astype(jnp.float32)
    far_high = swap(far[half:].astype(low), "tensor", 2).astype(jnp.float32)
    two = jnp.concatenate([two[:half] + far_low, two[half:]], axis=0).astype(low)
    one = jnp.concatenate([one[:half], one[half:] + far_high], axis=0).astype(low)
    from_one = swap(one, "tensor", 1).astype(jnp.float32)
    from_two = swap(two, "tensor", 2).astype(jnp.float32)
    if also:
        own = tie(own, *also)
    return own + from_one + from_two


def bits_of(axis):
    count = lax.axis_size(axis)
    return [1 << k for k in range(count.bit_length() - 1)]


def spread_columns(values):
    rows, cols = values.shape
    sides = [("dp", b) for b in reversed(bits_of("dp"))]
    sides += [("tensor", b) for b in reversed(bits_of("tensor"))]
    for axis, bit in sides:
        other = swap(values, axis, bit)
        high = (lax.axis_index(axis) & bit) != 0
        values = jnp.stack([jnp.where(high, other, values), jnp.where(high, values, other)])
    count = len(sides)
    order = (count,) + tuple(reversed(range(count))) + (count + 1,)
    return values.transpose(order).reshape(rows, -1)


def fold_columns(values):
    sides = [("dp", b) for b in reversed(bits_of("dp"))]
    sides += [("tensor", b) for b in reversed(bits_of("tensor"))]
    count = len(sides)
    rows = values.shape[0]
    values = values.reshape((rows,) + (2,) * count + (-1,))
    order = tuple(reversed(range(1, count + 1))) + (0, count + 1)
    values = values.transpose(order)
    for axis, bit in reversed(sides):
        high = (lax.axis_index(axis) & bit) != 0
        kept = jnp.where(high, values[1], values[0])
        given = jnp.where(high, values[0], values[1])
        values = kept + swap(given, axis, bit)
    return values


def fold_grad(values, dim):
    low = values.astype(jnp.bfloat16)
    return lax.psum_scatter(low, "dp", scatter_dimension=dim, tiled=True).astype(jnp.float32)


def local(tokens, w_qkv, w_out, w_up, w_down, w_ada, b_ada, timesteps, image_len, cotangent):
    n_tensor = lax.axis_size("tensor")
    n_data = lax.axis_size("dp")
    rows_dev = tokens.shape[0]
    tok_dev = rows_dev * n_tensor
    total_tok = tok_dev * n_data
    shift_pos = LONG // 32
    heads_local = w_qkv.shape[1] // (3 * HD)
    head_cols = heads_local * HD
    n_images = image_len.shape[0]
    data_idx = lax.axis_index("dp")
    tensor_idx = lax.axis_index("tensor")
    row_start = (data_idx * n_tensor + tensor_idx) * rows_dev
    row_pos = jnp.mod(row_start + jnp.arange(rows_dev, dtype=jnp.int32) + shift_pos, total_tok)
    seg_rows = segment_of(row_pos, image_len)
    ext_start = data_idx * tok_dev - tok_dev + shift_pos
    ext_pos = ext_start + jnp.arange(3 * tok_dev, dtype=jnp.int32)
    laps = (ext_pos >= total_tok).astype(jnp.int32) - (ext_pos < 0).astype(jnp.int32)
    seg_ext = segment_of(ext_pos - laps * total_tok, image_len) + laps * n_images
    seg_own = seg_ext[tok_dev : 2 * tok_dev].reshape(n_tensor, rows_dev)
    seg_tiles = seg_ext.reshape(3 * n_tensor, rows_dev)
    before = seg_tiles[:, -1][None, :] < seg_own[:, 0][:, None]
    reached = seg_tiles[:, 0][None, :] <= seg_own[:, -1][:, None]
    first_tile = jnp.sum(before.astype(jnp.int32), axis=1, dtype=jnp.int32)
    end_tile = jnp.sum(reached.astype(jnp.int32), axis=1, dtype=jnp.int32)
    scalars = jnp.concatenate([tensor_idx[None].astype(jnp.int32), first_tile, end_tile])
    seg_k = seg_ext[:, None]
    seg_q = seg_own[:, None, :]
    full_qkv = lax.all_gather(w_qkv, "dp", axis=0, tiled=True)
    full_out = lax.all_gather(w_out, "dp", axis=1, tiled=True)
    freq = frequency_table(timesteps, w_ada.shape[0])
    mod_cols = jnp.dot(freq, w_ada, precision=highest) + b_ada[None, :]
    modulation = spread_columns(mod_cols)
    image_ids = jnp.arange(n_images, dtype=jnp.int32)[None, :]
    onehot_rows = (seg_rows[:, None] == image_ids).astype(jnp.float32)
    mod_rows = jnp.dot(onehot_rows, modulation, precision=highest)
    width = modulation.shape[1] // 4
    scale_one = mod_rows[:, 0:width]
    shift_one = mod_rows[:, width : 2 * width]
    scale_two = mod_rows[:, 2 * width : 3 * width]
    shift_two = mod_rows[:, 3 * width : 4 * width]
    inputs_f = tokens.astype(jnp.float32)
    normed_one = norm_mod(inputs_f, scale_one, shift_one).astype(jnp.bfloat16)
    normed_full = spread_rows(normed_one)
    qkv = jnp.dot(normed_full, full_qkv, preferred_element_type=jnp.float32).astype(jnp.bfloat16)
    pair_rows = qkv.reshape(tok_dev, heads_local, 3, HD)[:, :, 1:].reshape(tok_dev, 2 * head_cols)
    forward, backward = ring("dp")
    low_pair = lax.ppermute(pair_rows, "dp", forward)
    high_pair = lax.ppermute(pair_rows, "dp", backward)
    grad_full = spread_rows(tie(cotangent, qkv))
    full_up = lax.all_gather(tie(w_up, low_pair, high_pair), "dp", axis=0, tiled=True)
    full_down = lax.all_gather(tie(w_down, low_pair, high_pair), "dp", axis=1, tiled=True)
    pair_ext = jnp.concatenate([low_pair, pair_rows, high_pair], axis=0)
    attn_lo, log_sums = attend(scalars, qkv, pair_ext, seg_k, seg_q, n_tensor)
    attn_lo = tie(attn_lo, grad_full)
    attn_part = jnp.dot(attn_lo, full_out, preferred_element_type=jnp.float32)
    branch = fold_rows(attn_part)
    mid_rows = inputs_f + branch
    normed_two = norm_mod(mid_rows, scale_two, shift_two).astype(jnp.bfloat16)
    normed_two_full = spread_rows(normed_two)
    up_rows = jnp.dot(normed_two_full, full_up, preferred_element_type=jnp.float32)
    act_rows = gelu_tanh(up_rows).astype(jnp.bfloat16)
    grad_rows = cotangent.astype(jnp.float32)
    grad_downw = jnp.einsum("tf,td->fd", act_rows, grad_full, preferred_element_type=jnp.float32)
    grad_downw = grad_downw.astype(jnp.bfloat16)
    d_act = jnp.einsum("td,fd->tf", grad_full, full_down, preferred_element_type=jnp.float32)
    gelu_pull = jax.vjp(gelu_tanh, up_rows)[1]
    d_up = gelu_pull(d_act)[0].astype(jnp.bfloat16)
    grad_upw = jnp.einsum("td,tf->df", normed_two_full, d_up, preferred_element_type=jnp.float32)
    grad_upw = grad_upw.astype(jnp.bfloat16)
    d_h2_part = jnp.einsum("tf,df->td", d_up, full_up, preferred_element_type=jnp.float32)
    d_h2 = fold_rows(d_h2_part, (grad_downw, grad_upw))
    norm_two_pull = jax.vjp(norm_mod, mid_rows, scale_two, shift_two)[1]
    d_mid, d_scale_two, d_shift_two = norm_two_pull(d_h2)
    d_mid = grad_rows + d_mid
    branch_full = spread_rows(d_mid.astype(jnp.bfloat16))
    grad_outw = jnp.einsum("tc,td->cd", attn_lo, branch_full, preferred_element_type=jnp.float32)
    d_attn = jnp.einsum("td,cd->tc", branch_full, full_out, preferred_element_type=jnp.float32)
    d_attn = d_attn.astype(jnp.bfloat16)
    mlp_part = jnp.dot(tie(act_rows, d_attn), full_down, preferred_element_type=jnp.float32)
    mlp_out = fold_rows(mlp_part)
    result = (mid_rows + mlp_out).astype(jnp.bfloat16)
    d_query, d_low, d_own, d_high = pull(
        scalars, qkv, pair_ext, seg_k, seg_q, log_sums, attn_lo, d_attn, n_tensor
    )
    from_prev = lax.ppermute(d_high, "dp", forward).astype(jnp.float32)
    from_next = lax.ppermute(d_low, "dp", backward).astype(jnp.float32)
    d_pair = (d_own + from_prev + from_next).astype(jnp.bfloat16)
    d_qkv = jnp.concatenate(
        [
            d_query.reshape(tok_dev, heads_local, 1, HD),
            d_pair.reshape(tok_dev, heads_local, 2, HD),
        ],
        axis=2,
    ).reshape(tok_dev, 3 * head_cols)
    grad_qkvw = jnp.einsum("td,tc->dc", normed_full, d_qkv, preferred_element_type=jnp.float32)
    d_h1_part = jnp.einsum("tc,dc->td", d_qkv, full_qkv, preferred_element_type=jnp.float32)
    d_h1 = fold_rows(d_h1_part)
    norm_one_pull = jax.vjp(norm_mod, inputs_f, scale_one, shift_one)[1]
    d_inputs, d_scale_one, d_shift_one = norm_one_pull(d_h1)
    grad_input = d_mid + d_inputs
    d_mod_rows = jnp.concatenate([d_scale_one, d_shift_one, d_scale_two, d_shift_two], axis=1)
    d_mod = jnp.dot(onehot_rows.T, d_mod_rows, precision=highest)
    d_mod_cols = fold_columns(d_mod)
    grad_adaw = jnp.dot(freq.T, d_mod_cols, precision=highest)
    grad_bias = jnp.sum(d_mod_cols, axis=0)
    grad_qkvw, grad_outw, grad_upw, grad_downw = (
        fold_grad(grad_qkvw, 0),
        fold_grad(grad_outw, 1),
        fold_grad(grad_upw, 0),
        fold_grad(grad_downw, 1),
    )
    return (result, grad_input, grad_qkvw, grad_outw, grad_upw, grad_downw, grad_adaw, grad_bias)


def solution(mesh):
    in_specs = (
        P(("dp", "tensor"), None),
        P("dp", "tensor"),
        P("tensor", "dp"),
        P("dp", "tensor"),
        P("tensor", "dp"),
        P(None, ("dp", "tensor")),
        P(("dp", "tensor")),
        P(),
        P(),
        P(("dp", "tensor"), None),
    )
    out_specs = (
        P(("dp", "tensor"), None),
        P(("dp", "tensor"), None),
        P("dp", "tensor"),
        P("tensor", "dp"),
        P("dp", "tensor"),
        P("tensor", "dp"),
        P(None, ("dp", "tensor")),
        P(("dp", "tensor")),
    )
    return jax.shard_map(local, mesh=mesh, in_specs=in_specs, out_specs=out_specs, check_vma=False)
```
